128 devices in a mesh: rows: 8 (over x, core), cols: 16 (over z, y).
Axes of the slice: x: 4, y: 4, z: 4, core: 2. Of those that a mesh axis runs over, the one named last changes fastest.
Arguments:
- blocks: bfloat16 [96, 96, 256, 256], P('rows', 'cols'), may hold values from -1.5 to 1.5
- pattern: int32 [96, 96], P('rows', 'cols'), may hold values 0 or 1
- pivot_inverse: bfloat16 [2, 256, 256], replicated, may hold values from -0.375 to 0.375
- right_sides: float32 [96, 3, 256], P('rows'), may hold values from -6 to 6
Outputs:
- factored: bfloat16 [96, 96, 256, 256], P('rows', 'cols')
- forward: float32 [96, 3, 256], P('rows')
The draws below stay inside these ranges and needn't reach their ends.
All inputs are finite; a program needn't handle non-finite values. No bound on the sum of `pattern` on one device may be relied on, other than what follows from the above.
Results may differ from the reference program's by a relative error of at most 0.0071.
Values may be sent and summed in bfloat16 or wider, within the bound.
A program may use at most 128 MiB of HBM per device.

```python
import jax
import jax.numpy as jnp
from jax import lax

B = 256
DIRS = 3
CB = 6
RB = 12
NB = 96
N_ROWS = 8
N_COLS = 16


def touch_ends(values, stream_key, smallest, top_value):
    shape = values.shape
    index_at = [jax.random.randint(jax.random.fold_in(stream_key, axis), (), 0, shape[axis]) for axis in range(len(shape))]
    values = values.at[tuple(index_at)].set(smallest)
    longest = shape.index(max(shape))
    index_at[longest] = (index_at[longest] + 1) % shape[longest]
    return values.at[tuple(index_at)].set(top_value)


def levels(own_key, shape, pieces, least, largest):
    level, own = 1.0, jax.random.fold_in(own_key, 6)
    for position, parts in pieces:
        draws = jnp.exp(jax.random.uniform(jax.random.fold_in(own, position), (parts,), jnp.float32, least / len(pieces), largest / len(pieces)))
        level = level * jnp.repeat(draws, shape[position] // parts).reshape([-1 if axis == position else 1 for axis in range(len(shape))])
    return level


def scatter_about(stream_key, shape, deviation, most, shards=(), kind=jnp.bfloat16):
    entries = deviation * jax.random.normal(stream_key, shape, jnp.float32)
    if shards:
        entries = entries * levels(stream_key, shape, shards, -0.22, 0.18)
    return jnp.clip(entries, -most, most).astype(kind)


def setup_inputs(seed: int = 0) -> dict:
    seeds = jax.random.split(jax.random.key(seed), 5)
    blocks = scatter_about(seeds[0], (NB, NB, B, B), 0.25, 1.5, ((0, 8), (1, 16)))
    pattern = touch_ends((jax.random.randint(seeds[1], (NB, NB), 0, 2) < 1).astype(jnp.int32), jax.random.fold_in(seeds[1], 1), 0, 1)
    pivot_inverse = scatter_about(seeds[2], (2, B, B), B ** -0.5, 0.375)
    right_sides = scatter_about(seeds[3], (NB, DIRS, B), 1.0, 6.0, ((0, 8),), jnp.float32)
    return {"blocks": blocks, "pattern": pattern, "pivot_inverse": pivot_inverse, "right_sides": right_sides}


def reference(blocks, pattern, pivot_inverse, right_sides):
    glob = jnp.arange(NB)
    row_src = ((glob % N_ROWS) * RB + glob // N_ROWS).astype(jnp.int32)
    col_src = ((glob % N_COLS) * CB + glob // N_COLS).astype(jnp.int32)
    store = jnp.arange(NB)
    row_back = ((store % RB) * N_ROWS + store // RB).astype(jnp.int32)
    col_back = ((store % CB) * N_COLS + store // CB).astype(jnp.int32)
    live = pattern[row_src][:, col_src] == 1
    matrix = blocks[row_src][:, col_src]
    matrix = jnp.where(live[:, :, None, None], matrix, jnp.zeros((), blocks.dtype))
    rhs = right_sides[row_src]
    lowers = []
    for k in range(2):
        column = matrix[:, k].astype(jnp.float32)
        lower = jnp.einsum("nab,bc->nac", column, pivot_inverse[k].astype(jnp.float32)).astype(jnp.bfloat16)
        lower = jnp.where((glob > k)[:, None, None], lower, jnp.zeros((), jnp.bfloat16))
        upper = jnp.where((glob > k)[:, None, None], matrix[k], jnp.zeros((), jnp.bfloat16))
        upper_f = upper.astype(jnp.float32)

        def one_row(packed):
            arow, lrow, prow = packed
            prod = jnp.einsum("ab,jbc->jac", lrow.astype(jnp.float32), upper_f)
            fresh = (arow.astype(jnp.float32) - prod).astype(jnp.bfloat16)
            return jnp.where(prow[:, None, None], fresh, arow)

        matrix = lax.map(one_row, (matrix, lower, live))
        newcol = jnp.where((glob > k)[:, None, None], lower, matrix[:, k])
        matrix = matrix.at[:, k].set(newcol)
        lowers.append(lower)
    first = rhs[0]
    rhs = rhs - jnp.einsum("nab,cb->nca", lowers[0].astype(jnp.float32), first, precision=lax.Precision.HIGHEST)
    second = rhs[1]
    rhs = rhs - jnp.einsum("nab,cb->nca", lowers[1].astype(jnp.float32), second, precision=lax.Precision.HIGHEST)
    factored = matrix[row_back][:, col_back]
    return factored, rhs[row_back]
```

```python
import functools

import jax
import jax.numpy as jnp
from jax import lax
from jax.experimental import pallas as pl
from jax.experimental.pallas import tpu as pltpu
from jax.sharding import PartitionSpec as P

MESH = pl.DeviceIdType.MESH
SIDE = 4

FORWARD = (
    (57344, 4864, 40705, 36864),
    (136, 34944, 16396, 17613),
    (3889, 48, 224, 2320),
    (70, 25671, 8194, 8736),
)
CHUNK = 64
LEAD = 2


def bit(table, position):
    return lax.rem(lax.shift_right_logical(jnp.int32(table), position), 2) == 1


def gather_kernel(
    blocks, pattern, rhs, panel, urow, pmask, umask, smask, ybuf,
    tree_send, tree_recv, local_sem, u_send, u_recv, sib_send, sib_recv,
    pm_send, pm_recv, tiny_send, tiny_recv, tsib_send, tsib_recv,
):
    row_blocks, col_blocks, side = blocks.shape[0], blocks.shape[1], blocks.shape[2]
    per = side // CHUNK
    steps = row_blocks * per // 4
    rows, cols = lax.axis_index("rows"), lax.axis_index("cols")
    x, core = rows // 2, lax.rem(rows, 2)
    z, y = cols // SIDE, lax.rem(cols, SIDE)
    other = 1 - core

    def at(new_x, new_core, new_z, new_y):
        return (new_x * 2 + new_core, new_z * SIDE + new_y)

    plane = (
        at(x, core, z, lax.rem(y + 1, SIDE)),
        at(x, core, lax.rem(z + 1, SIDE), y),
        at(x, core, z, lax.rem(y + 3, SIDE)),
        at(x, core, lax.rem(z + 3, SIDE), y),
    )
    along = at(lax.rem(x + 1 + 2 * core, SIDE), core, z, y)
    against = at(lax.rem(x + 3 + 2 * core, SIDE), core, z, y)
    sibling = at(x, other, z, y)
    hop = jnp.where(core == 0, x, lax.rem(SIDE - x, SIDE))
    head, passes = hop == 0, hop < SIDE - 1

    barrier = pltpu.get_barrier_semaphore()
    for peer in (*plane, along, against, sibling):
        pl.semaphore_signal(barrier, inc=1, device_id=peer, device_id_type=MESH)

    is_root, sends = [], []
    for p in range(2):
        position = lax.rem(y - p + SIDE, SIDE) * 4 + z
        is_root.append(cols == p)
        sends.append([[bit(FORWARD[k][d], position) for d in range(4)] for k in range(4)])
    pl.semaphore_wait(barrier, 7)

    def remote(src, dst, send, recv, to):
        return pltpu.make_async_remote_copy(
            src_ref=src, dst_ref=dst, send_sem=send, recv_sem=recv, device_id=to, device_id_type=MESH
        )

    def on_tree(p, k, src, dst, recv, send_of):
        for d in range(4):

            @pl.when(sends[p][k][d])
            def _():
                remote(src, dst, send_of(d), recv, plane[d]).start()

    def chunk_send(p, k, step, from_hbm):
        g = 4 * step + k
        dst = panel.at[p, g]
        if from_hbm:
            src = blocks.at[g // per, 0, pl.ds(pl.multiple_of(lax.rem(g, per) * CHUNK, CHUNK), CHUNK)]
        else:
            src = dst
        on_tree(p, k, src, dst, tree_recv.at[p, g], lambda d: tree_send.at[p, k, d])

    for p in range(2):

        @pl.when(is_root[p])
        def _():
            on_tree(p, 0, pattern, pmask.at[p], pm_recv.at[p], lambda d: pm_send.at[p, d])
            for step in range(LEAD):
                for k in range(4):
                    chunk_send(p, k, step, True)
            for i in range(row_blocks):
                for part in range(per):
                    pltpu.make_async_copy(
                        blocks.at[i, 0, pl.ds(part * CHUNK, CHUNK)], panel.at[p, i * per + part], local_sem.at[0]
                    ).start()
            pltpu.make_async_copy(pattern, pmask.at[p], local_sem.at[1]).start()

    @pl.when(head)
    def _():
        remote(pattern, umask.at[core], tiny_send.at[0, 0], tiny_recv.at[0], along).start()
        remote(pattern, umask.at[core], tsib_send.at[0], tsib_recv.at[0], sibling).start()
        remote(rhs.at[0], ybuf.at[core], tiny_send.at[0, 1], tiny_recv.at[1], along).start()
        remote(rhs.at[0], ybuf.at[core], tsib_send.at[1], tsib_recv.at[1], sibling).start()
        for j in range(col_blocks):
            remote(blocks.at[0, j], urow.at[core, j], u_send.at[j], u_recv.at[j], along).start()
            remote(blocks.at[0, j], urow.at[core, j], sib_send.at[j], sib_recv.at[j], sibling).start()
        for j in range(col_blocks):
            pltpu.make_async_copy(blocks.at[0, j], urow.at[core, j], local_sem.at[2]).start()
        pltpu.make_async_copy(pattern, umask.at[core], local_sem.at[3]).start()
        pltpu.make_async_copy(rhs.at[0], ybuf.at[core], local_sem.at[4]).start()

    for p in range(2):

        @pl.when(is_root[p])
        def _():
            whole = pltpu.make_async_copy(panel.at[p], panel.at[p], local_sem.at[0])
            whole.wait()
            pltpu.make_async_copy(pattern, pmask.at[p], local_sem.at[1]).wait()

        @pl.when(jnp.logical_not(is_root[p]))
        def _():
            remote(pattern, pmask.at[p], pm_send.at[p, 0], pm_recv.at[p], along).wait_recv()
            on_tree(p, 0, pmask.at[p], pmask.at[p], pm_recv.at[p], lambda d: pm_send.at[p, d])

    @pl.when(head)
    def _():
        for p in range(2):

            @pl.when(core == 1 - p)
            def _():
                remote(pmask.at[p], smask.at[core], tiny_send.at[0, 2], tiny_recv.at[2], along).start()
                remote(pmask.at[p], smask.at[core], tsib_send.at[2], tsib_recv.at[2], sibling).start()
                pltpu.make_async_copy(pmask.at[p], smask.at[core], local_sem.at[5]).start()

    def forward_tiny():
        for n, (src, dst) in enumerate(((umask, umask), (ybuf, ybuf), (smask, smask))):
            mine = dst.at[core]
            remote(mine, mine, tiny_send.at[0, n], tiny_recv.at[n], along).wait_recv()

            @pl.when(passes)
            def _():
                remote(mine, mine, tiny_send.at[0, n], tiny_recv.at[n], along).start()

            remote(mine, mine, tsib_send.at[n], tsib_recv.at[n], sibling).start()

    def forward_pivot(j):
        mine = urow.at[core, j]
        remote(mine, mine, u_send.at[j], u_recv.at[j], along).wait_recv()

        @pl.when(passes)
        def _():
            remote(mine, mine, u_send.at[j], u_recv.at[j], along).start()

        remote(mine, mine, sib_send.at[j], sib_recv.at[j], sibling).start()

    def one_step(step, carry):
        for p in range(2):

            @pl.when(jnp.logical_and(is_root[p], step + LEAD < steps))
            def _():
                for k in range(4):
                    chunk_send(p, k, step + LEAD, True)

        for k in range(4):
            for p in range(2):

                @pl.when(jnp.logical_not(is_root[p]))
                def _():
                    g = 4 * step + k
                    here = panel.at[p, g]
                    remote(here, here, tree_send.at[p, k, 0], tree_recv.at[p, g], along).wait_recv()
                    chunk_send(p, k, step, False)

        @pl.when(jnp.logical_and(head, step == 0))
        def _():
            for p in range(2):

                @pl.when(core == 1 - p)
                def _():
                    for part in range(per):
                        src = panel.at[p, part]
                        dst = urow.at[core, col_blocks, pl.ds(part * CHUNK, CHUNK)]
                        remote(src, dst, u_send.at[col_blocks + part], u_recv.at[col_blocks + part], along).start()
                        remote(src, dst, sib_send.at[col_blocks + part], sib_recv.at[col_blocks + part], sibling).start()
                        pltpu.make_async_copy(src, dst, local_sem.at[6]).start()

        @pl.when(jnp.logical_not(head))
        def _():
            @pl.when(step < col_blocks)
            def _():
                forward_pivot(step)

            @pl.when(step == col_blocks)
            def _():
                forward_tiny()
                for part in range(per):
                    mine = urow.at[core, col_blocks, pl.ds(part * CHUNK, CHUNK)]
                    n = col_blocks + part
                    remote(mine, mine, u_send.at[n], u_recv.at[n], along).wait_recv()

                    @pl.when(passes)
                    def _():
                        remote(mine, mine, u_send.at[n], u_recv.at[n], along).start()

                    remote(mine, mine, sib_send.at[n], sib_recv.at[n], sibling).start()

        return carry

    lax.fori_loop(0, steps, one_step, 0)

    for n, ref in enumerate((umask, ybuf, smask)):
        theirs = ref.at[other]
        remote(theirs, theirs, tsib_send.at[n], tsib_recv.at[n], sibling).wait_recv()
        remote(theirs, theirs, tsib_send.at[n], tsib_recv.at[n], sibling).wait_send()

        @pl.when(passes)
        def _():
            remote(theirs, theirs, tiny_send.at[0, n], tiny_recv.at[n], along).wait_send()

    for n in range(col_blocks + per):
        if n < col_blocks:
            theirs = urow.at[other, n]
        else:
            theirs = urow.at[other, col_blocks, pl.ds((n - col_blocks) * CHUNK, CHUNK)]
        remote(theirs, theirs, sib_send.at[n], sib_recv.at[n], sibling).wait_recv()
        remote(theirs, theirs, sib_send.at[n], sib_recv.at[n], sibling).wait_send()

        @pl.when(passes)
        def _():
            remote(theirs, theirs, u_send.at[n], u_recv.at[n], along).wait_send()

    @pl.when(head)
    def _():
        pltpu.make_async_copy(
            urow.at[core, pl.ds(0, col_blocks)], urow.at[core, pl.ds(0, col_blocks)], local_sem.at[2]
        ).wait()
        pltpu.make_async_copy(pattern, umask.at[core], local_sem.at[3]).wait()
        pltpu.make_async_copy(rhs.at[0], ybuf.at[core], local_sem.at[4]).wait()
        pltpu.make_async_copy(smask.at[core], smask.at[core], local_sem.at[5]).wait()
        pltpu.make_async_copy(urow.at[core, col_blocks], urow.at[core, col_blocks], local_sem.at[6]).wait()

    for p in range(2):
        for d in range(4):

            @pl.when(sends[p][0][d])
            def _():
                remote(pmask.at[p], pmask.at[p], pm_send.at[p, d], pm_recv.at[p], plane[d]).wait_send()

            for k in range(4):

                @pl.when(sends[p][k][d])
                def _():
                    part = panel.at[p, pl.ds(0, steps)]
                    remote(part, part, tree_send.at[p, k, d], tree_recv.at[p, 0], plane[d]).wait_send()


def gather(blocks, pattern, rhs):
    row_blocks, col_blocks, side = blocks.shape[:3]
    per = side // CHUNK
    dma = pltpu.SemaphoreType.DMA
    out_shape = (
        jax.ShapeDtypeStruct((2, row_blocks * per, CHUNK, side), jnp.bfloat16),
        jax.ShapeDtypeStruct((2, col_blocks + 1, side, side), jnp.bfloat16),
        jax.ShapeDtypeStruct((2, *pattern.shape), jnp.int32),
        jax.ShapeDtypeStruct((2, *pattern.shape), jnp.int32),
        jax.ShapeDtypeStruct((2, *pattern.shape), jnp.int32),
        jax.ShapeDtypeStruct((2, *rhs.shape[1:]), jnp.float32),
    )
    panel, urow, pmask, umask, smask, ybuf = pl.pallas_call(
        gather_kernel,
        out_shape=out_shape,
        in_specs=[pl.BlockSpec(memory_space=pl.ANY)] * 3,
        out_specs=[pl.BlockSpec(memory_space=pltpu.VMEM)] * 6,
        scratch_shapes=[
            dma((2, 4, 4)), dma((2, row_blocks * per)), dma((7,)),
            dma((col_blocks + per,)), dma((col_blocks + per,)),
            dma((col_blocks + per,)), dma((col_blocks + per,)),
            dma((2, 4)), dma((2,)), dma((1, 3)), dma((3,)), dma((3,)), dma((3,)),
        ],
        compiler_params=pltpu.CompilerParams(
            collective_id=0, has_side_effects=True, vmem_limit_bytes=16 * 2**20
        ),
        name="gather",
    )(blocks, pattern, rhs)
    return panel.reshape(2, row_blocks, side, side), urow, pmask, umask, smask, ybuf


def pieces(y):
    high = y.astype(jnp.bfloat16)
    rest = y - high.astype(jnp.float32)
    middle = rest.astype(jnp.bfloat16)
    low = (rest - middle.astype(jnp.float32)).astype(jnp.bfloat16)
    return high, middle, low


def matvec(stack, lower):
    return lax.dot_general(stack, lower, (((1,), (1,)), ((), ())), preferred_element_type=jnp.float32)


def update_kernel(
    pattern, pmask, umask, smask, blocks, panel, urow, pivots, ybuf, rhs, out, forward, upper, corner, ystack,
):
    i = pl.program_id(0)
    col_blocks, side = blocks.shape[1], blocks.shape[2]
    rows, cols = lax.axis_index("rows"), lax.axis_index("cols")
    row = i * 8 + rows
    f32, bf16 = jnp.float32, jnp.bfloat16

    def product(left, right):
        return jnp.dot(left, right, preferred_element_type=f32)

    def keep(flag, value):
        return jnp.where(flag, value, jnp.zeros_like(value))

    dirs = rhs.shape[1]

    @pl.when(i == 0)
    def _():
        corner[...] = keep(smask[0, 0, 0] == 1, urow[0, col_blocks])
        lower_one = product(keep(smask[1, 0, 0] == 1, urow[1, col_blocks]), pivots[0]).astype(bf16)
        for j in range(col_blocks):
            where = pl.ds(j * side, side)
            first = keep(jnp.logical_and(umask[0, 0, j] == 1, j * 16 + cols > 0), urow[0, j])
            second = (urow[1, j].astype(f32) - product(lower_one, first)).astype(bf16)
            upper[pl.ds(0, side), where] = first
            upper[pl.ds(side, side), where] = keep(
                jnp.logical_and(umask[1, 0, j] == 1, j * 16 + cols > 1), second
            )
        ystack[...] = jnp.zeros_like(ystack)
        for n, piece in enumerate(pieces(ybuf[0])):
            ystack[pl.ds(8 * n, dirs), pl.ds(0, side)] = piece.astype(f32)
        moved = matvec(ystack[:, pl.ds(0, side)].astype(bf16), lower_one)
        taken = moved[0:dirs] + moved[8 : 8 + dirs] + moved[16 : 16 + dirs]
        for n, piece in enumerate(pieces(ybuf[1] - taken)):
            ystack[pl.ds(8 * n, dirs), pl.ds(side, side)] = piece.astype(f32)

    first = product(panel[0, 0], pivots[0]).astype(bf16)
    first = keep(jnp.logical_and(pmask[0, i, 0] == 1, row > 0), first)
    schur = (panel[1, 0].astype(f32) - product(first, corner[...])).astype(bf16)
    second = product(schur, pivots[1]).astype(bf16)
    second = keep(jnp.logical_and(pmask[1, i, 0] == 1, row > 1), second)
    lower = jnp.concatenate([first, second], axis=1)
    for j in range(col_blocks):
        prod = product(lower, upper[:, pl.ds(j * side, side)])
        fresh = (blocks[0, j].astype(f32) - prod).astype(bf16)
        out[0, j] = keep(pattern[i, j] == 1, fresh)

    @pl.when(jnp.logical_and(cols == 0, row > 0))
    def _():
        out[0, 0] = first

    @pl.when(jnp.logical_and(cols == 1, row > 1))
    def _():
        out[0, 0] = second

    moved = matvec(ystack[...].astype(bf16), lower)
    forward[0] = rhs[0] - (moved[0:dirs] + moved[8 : 8 + dirs] + moved[16 : 16 + dirs])


def update(blocks, pattern, pivots, rhs, panel, urow, pmask, umask, smask, ybuf):
    row_blocks, col_blocks, side = blocks.shape[:3]
    dirs = rhs.shape[1]
    smem = pl.BlockSpec(memory_space=pltpu.SMEM)
    whole = lambda shape: pl.BlockSpec(shape, lambda i: (0,) * len(shape), pipeline_mode=pl.Buffered(1))
    return pl.pallas_call(
        update_kernel,
        grid=(row_blocks,),
        out_shape=(
            jax.ShapeDtypeStruct(blocks.shape, blocks.dtype),
            jax.ShapeDtypeStruct(rhs.shape, rhs.dtype),
        ),
        in_specs=[
            smem, smem, smem, smem,
            pl.BlockSpec((1, col_blocks, side, side), lambda i: (i, 0, 0, 0)),
            pl.BlockSpec((2, 1, side, side), lambda i: (0, i, 0, 0)),
            whole(urow.shape),
            whole(pivots.shape),
            whole(ybuf.shape),
            pl.BlockSpec((1, dirs, side), lambda i: (i, 0, 0)),
        ],
        out_specs=(
            pl.BlockSpec((1, col_blocks, side, side), lambda i: (i, 0, 0, 0)),
            pl.BlockSpec((1, dirs, side), lambda i: (i, 0, 0)),
        ),
        scratch_shapes=[
            pltpu.VMEM((2 * side, col_blocks * side), jnp.bfloat16),
            pltpu.VMEM((side, side), jnp.bfloat16),
            pltpu.VMEM((32, 2 * side), jnp.float32),
        ],
        compiler_params=pltpu.CompilerParams(vmem_limit_bytes=32 * 2**20),
        name="update",
    )(pattern, pmask, umask, smask, blocks, panel, urow, pivots, ybuf, rhs)


def on_device(blocks, pattern, pivot_inverse, right_sides):
    gathered = gather(blocks, pattern, right_sides)
    return update(blocks, pattern, pivot_inverse, right_sides, *gathered)


def solution(mesh):
    return jax.shard_map(
        on_device,
        mesh=mesh,
        in_specs=(P("rows", "cols", None, None), P("rows", "cols"), P(), P("rows", None, None)),
        out_specs=(P("rows", "cols", None, None), P("rows", None, None)),
        check_vma=False,
    )
```

```python
import functools

import jax
import jax.numpy as jnp
from jax import lax
from jax.experimental import pallas as pl
from jax.experimental.pallas import tpu as pltpu
from jax.sharding import PartitionSpec as P

MESH = pl.DeviceIdType.MESH
SIDE = 4

FORWARD = (
    (57344, 4864, 40705, 36864),
    (136, 34944, 16396, 17613),
    (3889, 48, 224, 2320),
    (70, 25671, 8194, 8736),
)
DEPTH = ((23130, 60186, 1252), (23130, 55510, 10016), (23130, 7146, 58372), (23130, 29308, 36224))
DEEPEST = 5
CHUNK = 64
LAG = 3
LAG_X = 2
LATE_X = 4


def bit(table, position):
    return lax.rem(lax.shift_right_logical(jnp.int32(table), position), 2) == 1


def gather_kernel(
    blocks, pattern, rhs, panel, urow, pmask, umask, smask, ybuf,
    tree_send, tree_recv, local_sem, u_send, u_recv, sib_send, sib_recv,
    pm_send, pm_recv, tiny_send, tiny_recv, tsib_send, tsib_recv,
):
    row_blocks, col_blocks, side = blocks.shape[0], blocks.shape[1], blocks.shape[2]
    per = side // CHUNK
    steps = row_blocks * per // 4
    rows, cols = lax.axis_index("rows"), lax.axis_index("cols")
    x, core = rows // 2, lax.rem(rows, 2)
    z, y = cols // SIDE, lax.rem(cols, SIDE)
    other = 1 - core

    def at(new_x, new_core, new_z, new_y):
        return (new_x * 2 + new_core, new_z * SIDE + new_y)

    plane = (
        at(x, core, z, lax.rem(y + 1, SIDE)),
        at(x, core, lax.rem(z + 1, SIDE), y),
        at(x, core, z, lax.rem(y + 3, SIDE)),
        at(x, core, lax.rem(z + 3, SIDE), y),
    )
    along = at(lax.rem(x + 1 + 2 * core, SIDE), core, z, y)
    against = at(lax.rem(x + 3 + 2 * core, SIDE), core, z, y)
    sibling = at(x, other, z, y)
    hop = jnp.where(core == 0, x, lax.rem(SIDE - x, SIDE))
    head, passes = hop == 0, hop < SIDE - 1

    barrier = pltpu.get_barrier_semaphore()
    for peer in (*plane, along, against, sibling):
        pl.semaphore_signal(barrier, inc=1, device_id=peer, device_id_type=MESH)

    is_root, sends, depth = [], [], []
    for p in range(2):
        position = lax.rem(y - p + SIDE, SIDE) * 4 + z
        is_root.append(cols == p)
        depth.append(
            [sum(bit(DEPTH[k][b], position).astype(jnp.int32) << b for b in range(3)) for k in range(4)]
        )
        sends.append([[bit(FORWARD[k][d], position) for d in range(4)] for k in range(4)])
    pl.semaphore_wait(barrier, 7)

    def remote(src, dst, send, recv, to):
        return pltpu.make_async_remote_copy(
            src_ref=src, dst_ref=dst, send_sem=send, recv_sem=recv, device_id=to, device_id_type=MESH
        )

    def on_tree(p, k, src, dst, recv, send_of):
        for d in range(4):

            @pl.when(sends[p][k][d])
            def _():
                remote(src, dst, send_of(d), recv, plane[d]).start()

    def chunk_send(p, k, step, from_hbm):
        g = 4 * step + k
        dst = panel.at[p, g]
        if from_hbm:
            src = blocks.at[g // per, 0, pl.ds(pl.multiple_of(lax.rem(g, per) * CHUNK, CHUNK), CHUNK)]
        else:
            src = dst
        on_tree(p, k, src, dst, tree_recv.at[p, g], lambda d: tree_send.at[p, k, d])

    for p in range(2):

        @pl.when(is_root[p])
        def _():
            for i in range(row_blocks):
                for part in range(per):
                    pltpu.make_async_copy(
                        blocks.at[i, 0, pl.ds(part * CHUNK, CHUNK)], panel.at[p, i * per + part], local_sem.at[0]
                    ).start()
            pltpu.make_async_copy(pattern, pmask.at[p], local_sem.at[1]).start()

    @pl.when(head)
    def _():
        remote(pattern, umask.at[core], tiny_send.at[0, 0], tiny_recv.at[0], along).start()
        remote(pattern, umask.at[core], tsib_send.at[0], tsib_recv.at[0], sibling).start()
        remote(rhs.at[0], ybuf.at[core], tiny_send.at[0, 1], tiny_recv.at[1], along).start()
        remote(rhs.at[0], ybuf.at[core], tsib_send.at[1], tsib_recv.at[1], sibling).start()
        for j in range(col_blocks):
            remote(blocks.at[0, j], urow.at[core, j], u_send.at[j], u_recv.at[j], along).start()
            remote(blocks.at[0, j], urow.at[core, j], sib_send.at[j], sib_recv.at[j], sibling).start()
        for j in range(col_blocks):
            pltpu.make_async_copy(blocks.at[0, j], urow.at[core, j], local_sem.at[2]).start()
        pltpu.make_async_copy(pattern, umask.at[core], local_sem.at[3]).start()
        pltpu.make_async_copy(rhs.at[0], ybuf.at[core], local_sem.at[4]).start()

    def forward_tiny():
        for n, (src, dst) in enumerate(((umask, umask), (ybuf, ybuf), (smask, smask))):
            mine = dst.at[core]
            remote(mine, mine, tiny_send.at[0, n], tiny_recv.at[n], along).wait_recv()

            @pl.when(passes)
            def _():
                remote(mine, mine, tiny_send.at[0, n], tiny_recv.at[n], along).start()

            remote(mine, mine, tsib_send.at[n], tsib_recv.at[n], sibling).start()

    def forward_pivot(j):
        mine = urow.at[core, j]
        remote(mine, mine, u_send.at[j], u_recv.at[j], along).wait_recv()

        @pl.when(passes)
        def _():
            remote(mine, mine, u_send.at[j], u_recv.at[j], along).start()

        remote(mine, mine, sib_send.at[j], sib_recv.at[j], sibling).start()

    def visit(p, k, step):
        @pl.when(is_root[p])
        def _():
            if k == 0:

                @pl.when(step == 0)
                def _():
                    on_tree(p, 0, pattern, pmask.at[p], pm_recv.at[p], lambda d: pm_send.at[p, d])

            chunk_send(p, k, step, True)

        @pl.when(jnp.logical_not(is_root[p]))
        def _():
            if k == 0:

                @pl.when(step == 0)
                def _():
                    remote(pattern, pmask.at[p], pm_send.at[p, 0], pm_recv.at[p], along).wait_recv()
                    on_tree(p, 0, pmask.at[p], pmask.at[p], pm_recv.at[p], lambda d: pm_send.at[p, d])

            g = 4 * step + k
            here = panel.at[p, g]
            remote(here, here, tree_send.at[p, k, 0], tree_recv.at[p, g], along).wait_recv()
            chunk_send(p, k, step, False)

    corner_slot = LAG * DEEPEST + 1

    def one_slot(slot, carry):
        for k in range(4):
            for p in range(2):
                step = slot - LAG * depth[p][k]

                @pl.when(jnp.logical_and(step >= 0, step < steps))
                def _():
                    visit(p, k, step)

        @pl.when(jnp.logical_and(head, slot == corner_slot))
        def _():
            for p in range(2):

                @pl.when(is_root[p])
                def _():
                    pltpu.make_async_copy(panel.at[p], panel.at[p], local_sem.at[0]).wait()
                    pltpu.make_async_copy(pattern, pmask.at[p], local_sem.at[1]).wait()

                @pl.when(core == 1 - p)
                def _():
                    remote(pmask.at[p], smask.at[core], tiny_send.at[0, 2], tiny_recv.at[2], along).start()
                    remote(pmask.at[p], smask.at[core], tsib_send.at[2], tsib_recv.at[2], sibling).start()
                    pltpu.make_async_copy(pmask.at[p], smask.at[core], local_sem.at[5]).start()
                    for part in range(per):
                        src = panel.at[p, part]
                        dst = urow.at[core, col_blocks, pl.ds(part * CHUNK, CHUNK)]
                        remote(src, dst, u_send.at[col_blocks + part], u_recv.at[col_blocks + part], along).start()
                        remote(src, dst, sib_send.at[col_blocks + part], sib_recv.at[col_blocks + part], sibling).start()
                        pltpu.make_async_copy(src, dst, local_sem.at[6]).start()

        @pl.when(jnp.logical_not(head))
        def _():
            j = slot - LATE_X - LAG_X * hop

            @pl.when(jnp.logical_and(j >= 0, j < col_blocks))
            def _():
                forward_pivot(j)

            @pl.when(j == corner_slot - LATE_X)
            def _():
                forward_tiny()
                for part in range(per):
                    mine = urow.at[core, col_blocks, pl.ds(part * CHUNK, CHUNK)]
                    n = col_blocks + part
                    remote(mine, mine, u_send.at[n], u_recv.at[n], along).wait_recv()

                    @pl.when(passes)
                    def _():
                        remote(mine, mine, u_send.at[n], u_recv.at[n], along).start()

                    remote(mine, mine, sib_send.at[n], sib_recv.at[n], sibling).start()

        return carry

    slots = max(steps + LAG * DEEPEST, corner_slot + LAG_X * (SIDE - 1) + 1, LATE_X + col_blocks + LAG_X * (SIDE - 1))
    lax.fori_loop(0, slots, one_slot, 0)

    for p in range(2):

        @pl.when(jnp.logical_and(is_root[p], jnp.logical_not(head)))
        def _():
            pltpu.make_async_copy(panel.at[p], panel.at[p], local_sem.at[0]).wait()
            pltpu.make_async_copy(pattern, pmask.at[p], local_sem.at[1]).wait()

    for n, ref in enumerate((umask, ybuf, smask)):
        theirs = ref.at[other]
        remote(theirs, theirs, tsib_send.at[n], tsib_recv.at[n], sibling).wait_recv()
        remote(theirs, theirs, tsib_send.at[n], tsib_recv.at[n], sibling).wait_send()

        @pl.when(passes)
        def _():
            remote(theirs, theirs, tiny_send.at[0, n], tiny_recv.at[n], along).wait_send()

    for n in range(col_blocks + per):
        if n < col_blocks:
            theirs = urow.at[other, n]
        else:
            theirs = urow.at[other, col_blocks, pl.ds((n - col_blocks) * CHUNK, CHUNK)]
        remote(theirs, theirs, sib_send.at[n], sib_recv.at[n], sibling).wait_recv()
        remote(theirs, theirs, sib_send.at[n], sib_recv.at[n], sibling).wait_send()

        @pl.when(passes)
        def _():
            remote(theirs, theirs, u_send.at[n], u_recv.at[n], along).wait_send()

    @pl.when(head)
    def _():
        pltpu.make_async_copy(
            urow.at[core, pl.ds(0, col_blocks)], urow.at[core, pl.ds(0, col_blocks)], local_sem.at[2]
        ).wait()
        pltpu.make_async_copy(pattern, umask.at[core], local_sem.at[3]).wait()
        pltpu.make_async_copy(rhs.at[0], ybuf.at[core], local_sem.at[4]).wait()
        pltpu.make_async_copy(smask.at[core], smask.at[core], local_sem.at[5]).wait()
        pltpu.make_async_copy(urow.at[core, col_blocks], urow.at[core, col_blocks], local_sem.at[6]).wait()

    for p in range(2):
        for d in range(4):

            @pl.when(sends[p][0][d])
            def _():
                remote(pmask.at[p], pmask.at[p], pm_send.at[p, d], pm_recv.at[p], plane[d]).wait_send()

            for k in range(4):

                @pl.when(sends[p][k][d])
                def _():
                    part = panel.at[p, pl.ds(0, steps)]
                    remote(part, part, tree_send.at[p, k, d], tree_recv.at[p, 0], plane[d]).wait_send()


def gather(blocks, pattern, rhs):
    row_blocks, col_blocks, side = blocks.shape[:3]
    per = side // CHUNK
    dma = pltpu.SemaphoreType.DMA
    out_shape = (
        jax.ShapeDtypeStruct((2, row_blocks * per, CHUNK, side), jnp.bfloat16),
        jax.ShapeDtypeStruct((2, col_blocks + 1, side, side), jnp.bfloat16),
        jax.ShapeDtypeStruct((2, *pattern.shape), jnp.int32),
        jax.ShapeDtypeStruct((2, *pattern.shape), jnp.int32),
        jax.ShapeDtypeStruct((2, *pattern.shape), jnp.int32),
        jax.ShapeDtypeStruct((2, *rhs.shape[1:]), jnp.float32),
    )
    panel, urow, pmask, umask, smask, ybuf = pl.pallas_call(
        gather_kernel,
        out_shape=out_shape,
        in_specs=[pl.BlockSpec(memory_space=pltpu.HBM)] * 3,
        out_specs=[pl.BlockSpec(memory_space=pltpu.VMEM)] * 6,
        scratch_shapes=[
            dma((2, 4, 4)), dma((2, row_blocks * per)), dma((7,)),
            dma((col_blocks + per,)), dma((col_blocks + per,)),
            dma((col_blocks + per,)), dma((col_blocks + per,)),
            dma((2, 4)), dma((2,)), dma((1, 3)), dma((3,)), dma((3,)), dma((3,)),
        ],
        compiler_params=pltpu.CompilerParams(
            collective_id=0, has_side_effects=True, vmem_limit_bytes=16 * 2**20
        ),
        name="gather",
    )(blocks, pattern, rhs)
    return panel.reshape(2, row_blocks, side, side), urow, pmask, umask, smask, ybuf


def pieces(y):
    high = y.astype(jnp.bfloat16)
    rest = y - high.astype(jnp.float32)
    middle = rest.astype(jnp.bfloat16)
    low = (rest - middle.astype(jnp.float32)).astype(jnp.bfloat16)
    return high, middle, low


def matvec(stack, lower):
    return lax.dot_general(stack, lower, (((1,), (1,)), ((), ())), preferred_element_type=jnp.float32)


GROUP = 2


def update_kernel(
    pattern, pmask, umask, smask, blocks, panel, urow, pivots, ybuf, rhs, out, forward, lower, upper, corner, ystack,
):
    j = pl.program_id(0)
    row_blocks, side = blocks.shape[0], blocks.shape[2]
    col_blocks = urow.shape[1] - 1
    rows, cols = lax.axis_index("rows"), lax.axis_index("cols")
    f32, bf16 = jnp.float32, jnp.bfloat16
    dirs = rhs.shape[1]
    groups = [range(n, n + GROUP) for n in range(0, row_blocks, GROUP)]

    def product(left, right):
        return jnp.dot(left, right, preferred_element_type=f32)

    def keep(flag, value):
        return jnp.where(flag, value, jnp.zeros_like(value))

    def part(group):
        return pl.ds(group[0] * side, GROUP * side)

    def stacked(p, group):
        return panel[p, pl.ds(group[0], GROUP)].reshape(GROUP * side, side)

    left, right = pl.ds(0, side), pl.ds(side, side)

    @pl.when(j == 0)
    def _():
        corner[...] = keep(smask[0, 0, 0] == 1, urow[0, col_blocks])
        for group in groups:
            value = product(stacked(0, group), pivots[0]).astype(bf16)
            for n, i in enumerate(group):
                flag = jnp.logical_and(pmask[0, 0, i] == 1, i * 8 + rows > 0)
                lower[pl.ds(i * side, side), left] = keep(flag, value[n * side : (n + 1) * side])
        for group in groups:
            value = stacked(1, group).astype(f32) - product(lower[part(group), left], corner[...])
            lower[part(group), right] = value.astype(bf16)
        for group in groups:
            value = product(lower[part(group), right], pivots[1]).astype(bf16)
            for n, i in enumerate(group):
                flag = jnp.logical_and(pmask[1, 0, i] == 1, i * 8 + rows > 1)
                lower[pl.ds(i * side, side), right] = keep(flag, value[n * side : (n + 1) * side])
        lower_one = product(keep(smask[1, 0, 0] == 1, urow[1, col_blocks]), pivots[0]).astype(bf16)
        for c in range(col_blocks):
            first = keep(jnp.logical_and(umask[0, c, 0] == 1, c * 16 + cols > 0), urow[0, c])
            second = (urow[1, c].astype(f32) - product(lower_one, first)).astype(bf16)
            upper[c, left] = first
            upper[c, right] = keep(jnp.logical_and(umask[1, c, 0] == 1, c * 16 + cols > 1), second)
        ystack[...] = jnp.zeros_like(ystack)
        for n, piece in enumerate(pieces(ybuf[0])):
            ystack[pl.ds(8 * n, dirs), left] = piece.astype(f32)
        moved = matvec(ystack[:, left].astype(bf16), lower_one)
        taken = moved[0:dirs] + moved[8 : 8 + dirs] + moved[16 : 16 + dirs]
        for n, piece in enumerate(pieces(ybuf[1] - taken)):
            ystack[pl.ds(8 * n, dirs), right] = piece.astype(f32)
        for i in range(row_blocks):
            moved = matvec(ystack[...].astype(bf16), lower[pl.ds(i * side, side)])
            forward[i] = rhs[i] - (moved[0:dirs] + moved[8 : 8 + dirs] + moved[16 : 16 + dirs])

    for group in groups:
        prod = product(lower[part(group)], upper[j])
        for n, i in enumerate(group):
            fresh = (blocks[i, 0].astype(f32) - prod[n * side : (n + 1) * side]).astype(bf16)
            out[i, 0] = keep(pattern[j, i] == 1, fresh)

    for p in range(2):

        @pl.when(jnp.logical_and(cols == p, j == 0))
        def _():
            for i in range(row_blocks):

                @pl.when(i * 8 + rows > p)
                def _():
                    out[i, 0] = lower[pl.ds(i * side, side), pl.ds(p * side, side)]


def update(blocks, pattern, pivots, rhs, panel, urow, pmask, umask, smask, ybuf):
    row_blocks, col_blocks, side = blocks.shape[:3]
    smem = pl.BlockSpec(memory_space=pltpu.SMEM)
    whole = lambda shape: pl.BlockSpec(shape, lambda j: (0,) * len(shape), pipeline_mode=pl.Buffered(1))
    column = pl.BlockSpec((row_blocks, 1, side, side), lambda j: (0, j, 0, 0))
    return pl.pallas_call(
        update_kernel,
        grid=(col_blocks,),
        out_shape=(
            jax.ShapeDtypeStruct(blocks.shape, blocks.dtype),
            jax.ShapeDtypeStruct(rhs.shape, rhs.dtype),
        ),
        in_specs=[
            smem, smem, smem, smem, column, whole(panel.shape), whole(urow.shape), whole(pivots.shape),
            whole(ybuf.shape), whole(rhs.shape),
        ],
        out_specs=(column, pl.BlockSpec(rhs.shape, lambda j: (0, 0, 0))),
        scratch_shapes=[
            pltpu.VMEM((row_blocks * side, 2 * side), jnp.bfloat16),
            pltpu.VMEM((col_blocks, 2 * side, side), jnp.bfloat16),
            pltpu.VMEM((side, side), jnp.bfloat16),
            pltpu.VMEM((32, 2 * side), jnp.float32),
        ],
        compiler_params=pltpu.CompilerParams(vmem_limit_bytes=32 * 2**20),
        name="update",
    )(pattern, pmask, umask, smask, blocks, panel, urow, pivots, ybuf, rhs)


def on_device(blocks, pattern, pivot_inverse, right_sides):
    pattern = pattern.T
    in_hbm = lambda array: pltpu.with_memory_space_constraint(array, pltpu.HBM)
    gathered = gather(in_hbm(blocks), in_hbm(pattern), in_hbm(right_sides))
    return update(blocks, pattern, pivot_inverse, right_sides, *gathered)


def solution(mesh):
    return jax.shard_map(
        on_device,
        mesh=mesh,
        in_specs=(P("rows", "cols", None, None), P("rows", "cols"), P(), P("rows", None, None)),
        out_specs=(P("rows", "cols", None, None), P("rows", None, None)),
        check_vma=False,
    )
```

```python
import functools

import jax
import jax.numpy as jnp
from jax import lax
from jax.experimental import pallas as pl
from jax.experimental.pallas import tpu as pltpu
from jax.sharding import PartitionSpec as P

MESH = pl.DeviceIdType.MESH
SIDE = 4

FORWARD = (
    ((34, 17511, 16390, 8736), (57344, 12288, 16129, 6400), (76, 34944, 32776, 50253), (3985, 784, 224, 144)),
    ((3985, 784, 224, 144), (34, 17511, 16390, 8736), (57344, 12288, 16129, 6400), (76, 34944, 32776, 50253)),
)
DEPTH = (
    ((23130, 29308, 36224), (23130, 60186, 1252), (23130, 55510, 10016), (23130, 7146, 58372)),
    ((23130, 7146, 58372), (23130, 29308, 36224), (23130, 60186, 1252), (23130, 55510, 10016)),
)
DEEPEST = 5
CHUNK = 64
LAG = 3
LAG_X = 2
LATE_X = 4


def bit(table, position):
    return lax.rem(lax.shift_right_logical(jnp.int32(table), position), 2) == 1


def gather_kernel(
    blocks, pattern, rhs, pivots_hbm, panel, urow, pmask, umask, smask, ybuf, pivots,
    tree_send, tree_recv, local_sem, u_send, u_recv, sib_send, sib_recv,
    pm_send, pm_recv, tiny_send, tiny_recv, tsib_send, tsib_recv,
):
    row_blocks, col_blocks, side = blocks.shape[0], blocks.shape[1], blocks.shape[2]
    per = side // CHUNK
    steps = row_blocks * per // 4
    rows, cols = lax.axis_index("rows"), lax.axis_index("cols")
    x, core = rows // 2, lax.rem(rows, 2)
    z, y = cols // SIDE, lax.rem(cols, SIDE)
    other = 1 - core

    def at(new_x, new_core, new_z, new_y):
        return (new_x * 2 + new_core, new_z * SIDE + new_y)

    plane = (
        at(x, core, z, lax.rem(y + 1, SIDE)),
        at(x, core, lax.rem(z + 1, SIDE), y),
        at(x, core, z, lax.rem(y + 3, SIDE)),
        at(x, core, lax.rem(z + 3, SIDE), y),
    )
    along = at(lax.rem(x + 1 + 2 * core, SIDE), core, z, y)
    against = at(lax.rem(x + 3 + 2 * core, SIDE), core, z, y)
    sibling = at(x, other, z, y)
    hop = jnp.where(core == 0, x, lax.rem(SIDE - x, SIDE))
    head, passes = hop == 0, hop < SIDE - 1

    load_pivots = pltpu.make_async_copy(pivots_hbm, pivots, local_sem.at[7])
    load_pivots.start()
    barrier = pltpu.get_barrier_semaphore()
    for peer in (*plane, along, against, sibling):
        pl.semaphore_signal(barrier, inc=1, device_id=peer, device_id_type=MESH)

    is_root, sends, depth = [], [], []
    for p in range(2):
        position = lax.rem(y - p + SIDE, SIDE) * 4 + z
        is_root.append(cols == p)
        depth.append(
            [sum(bit(DEPTH[p][k][b], position).astype(jnp.int32) << b for b in range(3)) for k in range(4)]
        )
        sends.append([[bit(FORWARD[p][k][d], position) for d in range(4)] for k in range(4)])
    pl.semaphore_wait(barrier, 7)

    def remote(src, dst, send, recv, to):
        return pltpu.make_async_remote_copy(
            src_ref=src, dst_ref=dst, send_sem=send, recv_sem=recv, device_id=to, device_id_type=MESH
        )

    def on_tree(p, k, src, dst, recv, send_of):
        for d in range(4):

            @pl.when(sends[p][k][d])
            def _():
                remote(src, dst, send_of(d), recv, plane[d]).start()

    def chunk_send(p, k, step, from_hbm):
        g = 4 * step + k
        dst = panel.at[p, g]
        if from_hbm:
            src = blocks.at[g // per, 0, pl.ds(pl.multiple_of(lax.rem(g, per) * CHUNK, CHUNK), CHUNK)]
        else:
            src = dst
        on_tree(p, k, src, dst, tree_recv.at[p, g], lambda d: tree_send.at[p, k, d])

    for p in range(2):

        @pl.when(is_root[p])
        def _():
            for i in range(row_blocks):
                for part in range(per):
                    pltpu.make_async_copy(
                        blocks.at[i, 0, pl.ds(part * CHUNK, CHUNK)], panel.at[p, i * per + part], local_sem.at[0]
                    ).start()
            pltpu.make_async_copy(pattern, pmask.at[p], local_sem.at[1]).start()

    @pl.when(head)
    def _():
        remote(pattern, umask.at[core], tiny_send.at[0, 0], tiny_recv.at[0], along).start()
        remote(pattern, umask.at[core], tsib_send.at[0], tsib_recv.at[0], sibling).start()
        remote(rhs.at[0], ybuf.at[core], tiny_send.at[0, 1], tiny_recv.at[1], along).start()
        remote(rhs.at[0], ybuf.at[core], tsib_send.at[1], tsib_recv.at[1], sibling).start()
        for j in range(col_blocks):
            remote(blocks.at[0, j], urow.at[core, j], u_send.at[j], u_recv.at[j], along).start()
            remote(blocks.at[0, j], urow.at[core, j], sib_send.at[j], sib_recv.at[j], sibling).start()
        for j in range(col_blocks):
            pltpu.make_async_copy(blocks.at[0, j], urow.at[core, j], local_sem.at[2]).start()
        pltpu.make_async_copy(pattern, umask.at[core], local_sem.at[3]).start()
        pltpu.make_async_copy(rhs.at[0], ybuf.at[core], local_sem.at[4]).start()

    def forward_tiny():
        for n, (src, dst) in enumerate(((umask, umask), (ybuf, ybuf), (smask, smask))):
            mine = dst.at[core]
            remote(mine, mine, tiny_send.at[0, n], tiny_recv.at[n], along).wait_recv()

            @pl.when(passes)
            def _():
                remote(mine, mine, tiny_send.at[0, n], tiny_recv.at[n], along).start()

            remote(mine, mine, tsib_send.at[n], tsib_recv.at[n], sibling).start()

    def forward_pivot(j):
        mine = urow.at[core, j]
        remote(mine, mine, u_send.at[j], u_recv.at[j], along).wait_recv()

        @pl.when(passes)
        def _():
            remote(mine, mine, u_send.at[j], u_recv.at[j], along).start()

        remote(mine, mine, sib_send.at[j], sib_recv.at[j], sibling).start()

    def visit(p, k, step):
        @pl.when(is_root[p])
        def _():
            if k == 0:

                @pl.when(step == 0)
                def _():
                    on_tree(p, 0, pattern, pmask.at[p], pm_recv.at[p], lambda d: pm_send.at[p, d])

            chunk_send(p, k, step, True)

        @pl.when(jnp.logical_not(is_root[p]))
        def _():
            if k == 0:

                @pl.when(step == 0)
                def _():
                    remote(pattern, pmask.at[p], pm_send.at[p, 0], pm_recv.at[p], along).wait_recv()
                    on_tree(p, 0, pmask.at[p], pmask.at[p], pm_recv.at[p], lambda d: pm_send.at[p, d])

            g = 4 * step + k
            here = panel.at[p, g]
            remote(here, here, tree_send.at[p, k, 0], tree_recv.at[p, g], along).wait_recv()
            chunk_send(p, k, step, False)

    corner_slot = LAG * DEEPEST + 1

    def one_slot(slot, carry):
        for k in range(4):
            for p in range(2):
                step = slot - LAG * depth[p][k]

                @pl.when(jnp.logical_and(step >= 0, step < steps))
                def _():
                    visit(p, k, step)

        @pl.when(jnp.logical_and(head, slot == corner_slot))
        def _():
            for p in range(2):

                @pl.when(is_root[p])
                def _():
                    pltpu.make_async_copy(panel.at[p], panel.at[p], local_sem.at[0]).wait()
                    pltpu.make_async_copy(pattern, pmask.at[p], local_sem.at[1]).wait()

                @pl.when(core == 1 - p)
                def _():
                    remote(pmask.at[p], smask.at[core], tiny_send.at[0, 2], tiny_recv.at[2], along).start()
                    remote(pmask.at[p], smask.at[core], tsib_send.at[2], tsib_recv.at[2], sibling).start()
                    pltpu.make_async_copy(pmask.at[p], smask.at[core], local_sem.at[5]).start()
                    for part in range(per):
                        src = panel.at[p, part]
                        dst = urow.at[core, col_blocks, pl.ds(part * CHUNK, CHUNK)]
                        remote(src, dst, u_send.at[col_blocks + part], u_recv.at[col_blocks + part], along).start()
                        remote(src, dst, sib_send.at[col_blocks + part], sib_recv.at[col_blocks + part], sibling).start()
                        pltpu.make_async_copy(src, dst, local_sem.at[6]).start()

        @pl.when(jnp.logical_not(head))
        def _():
            j = slot - LATE_X - LAG_X * hop

            @pl.when(jnp.logical_and(j >= 0, j < col_blocks))
            def _():
                forward_pivot(j)

            @pl.when(j == corner_slot - LATE_X)
            def _():
                forward_tiny()
                for part in range(per):
                    mine = urow.at[core, col_blocks, pl.ds(part * CHUNK, CHUNK)]
                    n = col_blocks + part
                    remote(mine, mine, u_send.at[n], u_recv.at[n], along).wait_recv()

                    @pl.when(passes)
                    def _():
                        remote(mine, mine, u_send.at[n], u_recv.at[n], along).start()

                    remote(mine, mine, sib_send.at[n], sib_recv.at[n], sibling).start()

        return carry

    slots = max(steps + LAG * DEEPEST, corner_slot + LAG_X * (SIDE - 1) + 1, LATE_X + col_blocks + LAG_X * (SIDE - 1))
    lax.fori_loop(0, slots, one_slot, 0)

    for p in range(2):

        @pl.when(jnp.logical_and(is_root[p], jnp.logical_not(head)))
        def _():
            pltpu.make_async_copy(panel.at[p], panel.at[p], local_sem.at[0]).wait()
            pltpu.make_async_copy(pattern, pmask.at[p], local_sem.at[1]).wait()

    load_pivots.wait()

    for n, ref in enumerate((umask, ybuf, smask)):
        theirs = ref.at[other]
        remote(theirs, theirs, tsib_send.at[n], tsib_recv.at[n], sibling).wait_recv()
        remote(theirs, theirs, tsib_send.at[n], tsib_recv.at[n], sibling).wait_send()

        @pl.when(passes)
        def _():
            remote(theirs, theirs, tiny_send.at[0, n], tiny_recv.at[n], along).wait_send()

    for n in range(col_blocks + per):
        if n < col_blocks:
            theirs = urow.at[other, n]
        else:
            theirs = urow.at[other, col_blocks, pl.ds((n - col_blocks) * CHUNK, CHUNK)]
        remote(theirs, theirs, sib_send.at[n], sib_recv.at[n], sibling).wait_recv()
        remote(theirs, theirs, sib_send.at[n], sib_recv.at[n], sibling).wait_send()

        @pl.when(passes)
        def _():
            remote(theirs, theirs, u_send.at[n], u_recv.at[n], along).wait_send()

    @pl.when(head)
    def _():
        pltpu.make_async_copy(
            urow.at[core, pl.ds(0, col_blocks)], urow.at[core, pl.ds(0, col_blocks)], local_sem.at[2]
        ).wait()
        pltpu.make_async_copy(pattern, umask.at[core], local_sem.at[3]).wait()
        pltpu.make_async_copy(rhs.at[0], ybuf.at[core], local_sem.at[4]).wait()
        pltpu.make_async_copy(smask.at[core], smask.at[core], local_sem.at[5]).wait()
        pltpu.make_async_copy(urow.at[core, col_blocks], urow.at[core, col_blocks], local_sem.at[6]).wait()

    for p in range(2):
        for d in range(4):

            @pl.when(sends[p][0][d])
            def _():
                remote(pmask.at[p], pmask.at[p], pm_send.at[p, d], pm_recv.at[p], plane[d]).wait_send()

            for k in range(4):

                @pl.when(sends[p][k][d])
                def _():
                    part = panel.at[p, pl.ds(0, steps)]
                    remote(part, part, tree_send.at[p, k, d], tree_recv.at[p, 0], plane[d]).wait_send()


def gather(blocks, pattern, rhs, pivots):
    row_blocks, col_blocks, side = blocks.shape[:3]
    per = side // CHUNK
    dma = pltpu.SemaphoreType.DMA
    out_shape = (
        jax.ShapeDtypeStruct((2, row_blocks * per, CHUNK, side), jnp.bfloat16),
        jax.ShapeDtypeStruct((2, col_blocks + 1, side, side), jnp.bfloat16),
        jax.ShapeDtypeStruct((2, *pattern.shape), jnp.int32),
        jax.ShapeDtypeStruct((2, *pattern.shape), jnp.int32),
        jax.ShapeDtypeStruct((2, *pattern.shape), jnp.int32),
        jax.ShapeDtypeStruct((2, *rhs.shape[1:]), jnp.float32),
        jax.ShapeDtypeStruct(pivots.shape, pivots.dtype),
    )
    panel, urow, pmask, umask, smask, ybuf, pivots = pl.pallas_call(
        gather_kernel,
        out_shape=out_shape,
        in_specs=[pl.BlockSpec(memory_space=pltpu.HBM)] * 4,
        out_specs=[pl.BlockSpec(memory_space=pltpu.VMEM)] * 7,
        scratch_shapes=[
            dma((2, 4, 4)), dma((2, row_blocks * per)), dma((8,)),
            dma((col_blocks + per,)), dma((col_blocks + per,)),
            dma((col_blocks + per,)), dma((col_blocks + per,)),
            dma((2, 4)), dma((2,)), dma((1, 3)), dma((3,)), dma((3,)), dma((3,)),
        ],
        compiler_params=pltpu.CompilerParams(
            collective_id=0, has_side_effects=True, vmem_limit_bytes=16 * 2**20
        ),
        name="gather",
    )(blocks, pattern, rhs, pivots)
    return panel.reshape(2, row_blocks, side, side), urow, pmask, umask, smask, ybuf, pivots


def pieces(y):
    high = y.astype(jnp.bfloat16)
    rest = y - high.astype(jnp.float32)
    middle = rest.astype(jnp.bfloat16)
    low = (rest - middle.astype(jnp.float32)).astype(jnp.bfloat16)
    return high, middle, low


def matvec(stack, lower):
    return lax.dot_general(stack, lower, (((1,), (1,)), ((), ())), preferred_element_type=jnp.float32)


GROUP = 2


def update_kernel(
    pattern, pmask, umask, smask, blocks, panel, urow, pivots, ybuf, rhs, out, forward,
    lower, upper, corner, ystack, solved, stage, out_sem, forward_sem,
):
    row_blocks, side = blocks.shape[0], blocks.shape[2]
    col_blocks = urow.shape[1] - 1
    rows, cols = lax.axis_index("rows"), lax.axis_index("cols")
    f32, bf16 = jnp.float32, jnp.bfloat16
    dirs = rhs.shape[1]
    groups = [range(n, n + GROUP) for n in range(0, row_blocks, GROUP)]

    def product(left, right):
        return jnp.dot(left, right, preferred_element_type=f32)

    def keep(flag, value):
        return jnp.where(flag, value, jnp.zeros_like(value))

    def part(group):
        return pl.ds(group[0] * side, GROUP * side)

    def stacked(p, group):
        return panel[p, pl.ds(group[0], GROUP)].reshape(GROUP * side, side)

    left, right = pl.ds(0, side), pl.ds(side, side)

    corner[...] = keep(smask[0, 0, 0] == 1, urow[0, col_blocks])
    for group in groups:
        value = product(stacked(0, group), pivots[0]).astype(bf16)
        for n, i in enumerate(group):
            flag = jnp.logical_and(pmask[0, 0, i] == 1, i * 8 + rows > 0)
            lower[pl.ds(i * side, side), left] = keep(flag, value[n * side : (n + 1) * side])
    for group in groups:
        value = stacked(1, group).astype(f32) - product(lower[part(group), left], corner[...])
        lower[part(group), right] = value.astype(bf16)
    for group in groups:
        value = product(lower[part(group), right], pivots[1]).astype(bf16)
        for n, i in enumerate(group):
            flag = jnp.logical_and(pmask[1, 0, i] == 1, i * 8 + rows > 1)
            lower[pl.ds(i * side, side), right] = keep(flag, value[n * side : (n + 1) * side])
    lower_one = product(keep(smask[1, 0, 0] == 1, urow[1, col_blocks]), pivots[0]).astype(bf16)
    for c in range(col_blocks):
        first = keep(jnp.logical_and(umask[0, c, 0] == 1, c * 16 + cols > 0), urow[0, c])
        second = (urow[1, c].astype(f32) - product(lower_one, first)).astype(bf16)
        upper[c, left] = first
        upper[c, right] = keep(jnp.logical_and(umask[1, c, 0] == 1, c * 16 + cols > 1), second)
    ystack[...] = jnp.zeros_like(ystack)
    for n, piece in enumerate(pieces(ybuf[0])):
        ystack[pl.ds(8 * n, dirs), left] = piece.astype(f32)
    moved = matvec(ystack[:, left].astype(bf16), lower_one)
    taken = moved[0:dirs] + moved[8 : 8 + dirs] + moved[16 : 16 + dirs]
    for n, piece in enumerate(pieces(ybuf[1] - taken)):
        ystack[pl.ds(8 * n, dirs), right] = piece.astype(f32)
    for i in range(row_blocks):
        moved = matvec(ystack[...].astype(bf16), lower[pl.ds(i * side, side)])
        solved[i] = rhs[i] - (moved[0:dirs] + moved[8 : 8 + dirs] + moved[16 : 16 + dirs])
    send_forward = pltpu.make_async_copy(solved, forward, forward_sem)
    send_forward.start()

    def send(j, group):
        rows_of = pl.ds(group[0], GROUP)
        pltpu.make_async_copy(stage.at[j % 2, rows_of], out.at[rows_of, j], out_sem.at[j % 2]).start()

    def sent(j):
        pltpu.make_async_copy(stage.at[j % 2], out.at[:, j], out_sem.at[j % 2]).wait()

    for j in range(col_blocks):
        if j >= 2:
            sent(j - 2)
        for group in groups:
            prod = product(lower[part(group)], upper[j])
            for n, i in enumerate(group):
                fresh = (blocks[i, j].astype(f32) - prod[n * side : (n + 1) * side]).astype(bf16)
                stage[j % 2, i] = keep(pattern[j, i] == 1, fresh)
            if j > 0:
                send(j, group)
        if j == 0:
            for p in range(2):

                @pl.when(cols == p)
                def _():
                    for i in range(row_blocks):

                        @pl.when(i * 8 + rows > p)
                        def _():
                            stage[0, i] = lower[pl.ds(i * side, side), pl.ds(p * side, side)]

            for group in groups:
                send(j, group)
    sent(col_blocks - 2)
    sent(col_blocks - 1)
    send_forward.wait()


def update(blocks, pattern, rhs, panel, urow, pmask, umask, smask, ybuf, pivots):
    row_blocks, col_blocks, side = blocks.shape[:3]
    smem, vmem = pl.BlockSpec(memory_space=pltpu.SMEM), pl.BlockSpec(memory_space=pltpu.VMEM)
    return pl.pallas_call(
        update_kernel,
        out_shape=(
            jax.ShapeDtypeStruct(blocks.shape, blocks.dtype),
            jax.ShapeDtypeStruct(rhs.shape, rhs.dtype),
        ),
        in_specs=[smem] * 4 + [vmem] * 6,
        out_specs=[pl.BlockSpec(memory_space=pltpu.HBM)] * 2,
        scratch_shapes=[
            pltpu.VMEM((row_blocks * side, 2 * side), jnp.bfloat16),
            pltpu.VMEM((col_blocks, 2 * side, side), jnp.bfloat16),
            pltpu.VMEM((side, side), jnp.bfloat16),
            pltpu.VMEM((32, 2 * side), jnp.float32),
            pltpu.VMEM(rhs.shape, rhs.dtype),
            pltpu.VMEM((2, row_blocks, side, side), jnp.bfloat16),
            pltpu.SemaphoreType.DMA((2,)),
            pltpu.SemaphoreType.DMA,
        ],
        compiler_params=pltpu.CompilerParams(vmem_limit_bytes=24 * 2**20),
        name="update",
    )(pattern, pmask, umask, smask, blocks, panel, urow, pivots, ybuf, rhs)


def on_device(blocks, pattern, pivot_inverse, right_sides):
    pattern = pattern.T
    in_hbm = lambda array: pltpu.with_memory_space_constraint(array, pltpu.HBM)
    gathered = gather(in_hbm(blocks), in_hbm(pattern), in_hbm(right_sides), in_hbm(pivot_inverse))
    return tuple(update(blocks, pattern, right_sides, *gathered))


def solution(mesh):
    return jax.shard_map(
        on_device,
        mesh=mesh,
        in_specs=(P("rows", "cols", None, None), P("rows", "cols"), P(), P("rows", None, None)),
        out_specs=(P("rows", "cols", None, None), P("rows", None, None)),
        check_vma=False,
    )
```

```python
import functools

import jax
import jax.numpy as jnp
from jax import lax
from jax.experimental import pallas as pl
from jax.experimental.pallas import tpu as pltpu
from jax.sharding import PartitionSpec as P

MESH = pl.DeviceIdType.MESH
SIDE = 4

FORWARD = (
    ((34, 17511, 16390, 8736), (57344, 12288, 16129, 6400), (76, 34944, 32776, 50253), (3985, 784, 224, 144)),
    ((3985, 784, 224, 144), (34, 17511, 16390, 8736), (57344, 12288, 16129, 6400), (76, 34944, 32776, 50253)),
)
DEPTH = (
    ((23130, 29308, 36224), (23130, 60186, 1252), (23130, 55510, 10016), (23130, 7146, 58372)),
    ((23130, 7146, 58372), (23130, 29308, 36224), (23130, 60186, 1252), (23130, 55510, 10016)),
)
DEEPEST = 5
CHUNK = 64
LAG = 3
LAG_X = 2
LATE_X = 4


def bit(table, position):
    return lax.rem(lax.shift_right_logical(jnp.int32(table), position), 2) == 1


def gather_kernel(
    blocks, pattern, rhs, pivots_hbm, panel, urow, pmask, umask, smask, ybuf, pivots,
    tree_send, tree_recv, local_sem, u_send, u_recv, sib_send, sib_recv,
    pm_send, pm_recv, tiny_send, tiny_recv, tsib_send, tsib_recv,
):
    row_blocks, col_blocks, side = blocks.shape[0], blocks.shape[1], blocks.shape[2]
    per = side // CHUNK
    steps = row_blocks * per // 4
    rows, cols = lax.axis_index("rows"), lax.axis_index("cols")
    x, core = rows // 2, lax.rem(rows, 2)
    z, y = cols // SIDE, lax.rem(cols, SIDE)
    other = 1 - core

    def at(new_x, new_core, new_z, new_y):
        return (new_x * 2 + new_core, new_z * SIDE + new_y)

    plane = (
        at(x, core, z, lax.rem(y + 1, SIDE)),
        at(x, core, lax.rem(z + 1, SIDE), y),
        at(x, core, z, lax.rem(y + 3, SIDE)),
        at(x, core, lax.rem(z + 3, SIDE), y),
    )
    along = at(lax.rem(x + 1 + 2 * core, SIDE), core, z, y)
    against = at(lax.rem(x + 3 + 2 * core, SIDE), core, z, y)
    sibling = at(x, other, z, y)
    hop = jnp.where(core == 0, x, lax.rem(SIDE - x, SIDE))
    head, passes = hop == 0, hop < SIDE - 1

    load_pivots = pltpu.make_async_copy(pivots_hbm, pivots, local_sem.at[7])
    load_pivots.start()
    barrier = pltpu.get_barrier_semaphore()
    for peer in (*plane, along, against, sibling):
        pl.semaphore_signal(barrier, inc=1, device_id=peer, device_id_type=MESH)

    is_root, sends, depth = [], [], []
    for p in range(2):
        position = lax.rem(y - p + SIDE, SIDE) * 4 + z
        is_root.append(cols == p)
        depth.append(
            [sum(bit(DEPTH[p][k][b], position).astype(jnp.int32) << b for b in range(3)) for k in range(4)]
        )
        sends.append([[bit(FORWARD[p][k][d], position) for d in range(4)] for k in range(4)])
    pl.semaphore_wait(barrier, 7)

    def remote(src, dst, send, recv, to):
        return pltpu.make_async_remote_copy(
            src_ref=src, dst_ref=dst, send_sem=send, recv_sem=recv, device_id=to, device_id_type=MESH
        )

    def on_tree(p, k, src, dst, recv, send_of):
        for d in range(4):

            @pl.when(sends[p][k][d])
            def _():
                remote(src, dst, send_of(d), recv, plane[d]).start()

    def chunk_send(p, k, step, from_hbm):
        g = 4 * step + k
        dst = panel.at[p, g]
        if from_hbm:
            src = blocks.at[g // per, 0, pl.ds(pl.multiple_of(lax.rem(g, per) * CHUNK, CHUNK), CHUNK)]
        else:
            src = dst
        on_tree(p, k, src, dst, tree_recv.at[p, g], lambda d: tree_send.at[p, k, d])

    for p in range(2):

        @pl.when(is_root[p])
        def _():
            for i in range(row_blocks):
                for part in range(per):
                    pltpu.make_async_copy(
                        blocks.at[i, 0, pl.ds(part * CHUNK, CHUNK)], panel.at[p, i * per + part], local_sem.at[0]
                    ).start()
            pltpu.make_async_copy(pattern, pmask.at[p], local_sem.at[1]).start()

    @pl.when(head)
    def _():
        remote(pattern, umask.at[core], tiny_send.at[0, 0], tiny_recv.at[0], along).start()
        remote(pattern, umask.at[core], tsib_send.at[0], tsib_recv.at[0], sibling).start()
        remote(rhs.at[0], ybuf.at[core], tiny_send.at[0, 1], tiny_recv.at[1], along).start()
        remote(rhs.at[0], ybuf.at[core], tsib_send.at[1], tsib_recv.at[1], sibling).start()
        for j in range(col_blocks):
            remote(blocks.at[0, j], urow.at[core, j], u_send.at[j], u_recv.at[j], along).start()
            remote(blocks.at[0, j], urow.at[core, j], sib_send.at[j], sib_recv.at[j], sibling).start()
        for j in range(col_blocks):
            pltpu.make_async_copy(blocks.at[0, j], urow.at[core, j], local_sem.at[2]).start()
        pltpu.make_async_copy(pattern, umask.at[core], local_sem.at[3]).start()
        pltpu.make_async_copy(rhs.at[0], ybuf.at[core], local_sem.at[4]).start()

    def forward_tiny():
        for n, (src, dst) in enumerate(((umask, umask), (ybuf, ybuf), (smask, smask))):
            mine = dst.at[core]
            remote(mine, mine, tiny_send.at[0, n], tiny_recv.at[n], along).wait_recv()

            @pl.when(passes)
            def _():
                remote(mine, mine, tiny_send.at[0, n], tiny_recv.at[n], along).start()

            remote(mine, mine, tsib_send.at[n], tsib_recv.at[n], sibling).start()

    def forward_pivot(j):
        mine = urow.at[core, j]
        remote(mine, mine, u_send.at[j], u_recv.at[j], along).wait_recv()

        @pl.when(passes)
        def _():
            remote(mine, mine, u_send.at[j], u_recv.at[j], along).start()

        remote(mine, mine, sib_send.at[j], sib_recv.at[j], sibling).start()

    def visit(p, k, step):
        @pl.when(is_root[p])
        def _():
            if k == 0:

                @pl.when(step == 0)
                def _():
                    on_tree(p, 0, pattern, pmask.at[p], pm_recv.at[p], lambda d: pm_send.at[p, d])

            chunk_send(p, k, step, True)

        @pl.when(jnp.logical_not(is_root[p]))
        def _():
            if k == 0:

                @pl.when(step == 0)
                def _():
                    remote(pattern, pmask.at[p], pm_send.at[p, 0], pm_recv.at[p], along).wait_recv()
                    on_tree(p, 0, pmask.at[p], pmask.at[p], pm_recv.at[p], lambda d: pm_send.at[p, d])

            g = 4 * step + k
            here = panel.at[p, g]
            remote(here, here, tree_send.at[p, k, 0], tree_recv.at[p, g], along).wait_recv()
            chunk_send(p, k, step, False)

    corner_slot = LAG * DEEPEST + 1

    def one_slot(slot, carry):
        for k in range(4):
            for p in range(2):
                step = slot - LAG * depth[p][k]

                @pl.when(jnp.logical_and(step >= 0, step < steps))
                def _():
                    visit(p, k, step)

        @pl.when(jnp.logical_and(head, slot == corner_slot))
        def _():
            for p in range(2):

                @pl.when(is_root[p])
                def _():
                    pltpu.make_async_copy(panel.at[p], panel.at[p], local_sem.at[0]).wait()
                    pltpu.make_async_copy(pattern, pmask.at[p], local_sem.at[1]).wait()

                @pl.when(core == 1 - p)
                def _():
                    remote(pmask.at[p], smask.at[core], tiny_send.at[0, 2], tiny_recv.at[2], along).start()
                    remote(pmask.at[p], smask.at[core], tsib_send.at[2], tsib_recv.at[2], sibling).start()
                    pltpu.make_async_copy(pmask.at[p], smask.at[core], local_sem.at[5]).start()
                    for part in range(per):
                        src = panel.at[p, part]
                        dst = urow.at[core, col_blocks, pl.ds(part * CHUNK, CHUNK)]
                        remote(src, dst, u_send.at[col_blocks + part], u_recv.at[col_blocks + part], along).start()
                        remote(src, dst, sib_send.at[col_blocks + part], sib_recv.at[col_blocks + part], sibling).start()
                        pltpu.make_async_copy(src, dst, local_sem.at[6]).start()

        @pl.when(jnp.logical_not(head))
        def _():
            j = slot - LATE_X - LAG_X * hop

            @pl.when(jnp.logical_and(j >= 0, j < col_blocks))
            def _():
                forward_pivot(j)

            @pl.when(j == corner_slot - LATE_X)
            def _():
                forward_tiny()
                for part in range(per):
                    mine = urow.at[core, col_blocks, pl.ds(part * CHUNK, CHUNK)]
                    n = col_blocks + part
                    remote(mine, mine, u_send.at[n], u_recv.at[n], along).wait_recv()

                    @pl.when(passes)
                    def _():
                        remote(mine, mine, u_send.at[n], u_recv.at[n], along).start()

                    remote(mine, mine, sib_send.at[n], sib_recv.at[n], sibling).start()

        return carry

    slots = max(steps + LAG * DEEPEST, corner_slot + LAG_X * (SIDE - 1) + 1, LATE_X + col_blocks + LAG_X * (SIDE - 1))
    lax.fori_loop(0, slots, one_slot, 0)

    for p in range(2):

        @pl.when(jnp.logical_and(is_root[p], jnp.logical_not(head)))
        def _():
            pltpu.make_async_copy(panel.at[p], panel.at[p], local_sem.at[0]).wait()
            pltpu.make_async_copy(pattern, pmask.at[p], local_sem.at[1]).wait()

    load_pivots.wait()

    for n, ref in enumerate((umask, ybuf, smask)):
        theirs = ref.at[other]
        remote(theirs, theirs, tsib_send.at[n], tsib_recv.at[n], sibling).wait_recv()
        remote(theirs, theirs, tsib_send.at[n], tsib_recv.at[n], sibling).wait_send()

        @pl.when(passes)
        def _():
            remote(theirs, theirs, tiny_send.at[0, n], tiny_recv.at[n], along).wait_send()

    for n in range(col_blocks + per):
        if n < col_blocks:
            theirs = urow.at[other, n]
        else:
            theirs = urow.at[other, col_blocks, pl.ds((n - col_blocks) * CHUNK, CHUNK)]
        remote(theirs, theirs, sib_send.at[n], sib_recv.at[n], sibling).wait_recv()
        remote(theirs, theirs, sib_send.at[n], sib_recv.at[n], sibling).wait_send()

        @pl.when(passes)
        def _():
            remote(theirs, theirs, u_send.at[n], u_recv.at[n], along).wait_send()

    @pl.when(head)
    def _():
        pltpu.make_async_copy(
            urow.at[core, pl.ds(0, col_blocks)], urow.at[core, pl.ds(0, col_blocks)], local_sem.at[2]
        ).wait()
        pltpu.make_async_copy(pattern, umask.at[core], local_sem.at[3]).wait()
        pltpu.make_async_copy(rhs.at[0], ybuf.at[core], local_sem.at[4]).wait()
        pltpu.make_async_copy(smask.at[core], smask.at[core], local_sem.at[5]).wait()
        pltpu.make_async_copy(urow.at[core, col_blocks], urow.at[core, col_blocks], local_sem.at[6]).wait()

    for p in range(2):
        for d in range(4):

            @pl.when(sends[p][0][d])
            def _():
                remote(pmask.at[p], pmask.at[p], pm_send.at[p, d], pm_recv.at[p], plane[d]).wait_send()

            for k in range(4):

                @pl.when(sends[p][k][d])
                def _():
                    part = panel.at[p, pl.ds(0, steps)]
                    remote(part, part, tree_send.at[p, k, d], tree_recv.at[p, 0], plane[d]).wait_send()


def gather(blocks, pattern, rhs, pivots):
    row_blocks, col_blocks, side = blocks.shape[:3]
    per = side // CHUNK
    dma = pltpu.SemaphoreType.DMA
    out_shape = (
        jax.ShapeDtypeStruct((2, row_blocks * per, CHUNK, side), jnp.bfloat16),
        jax.ShapeDtypeStruct((2, col_blocks + 1, side, side), jnp.bfloat16),
        jax.ShapeDtypeStruct((2, *pattern.shape), jnp.int32),
        jax.ShapeDtypeStruct((2, *pattern.shape), jnp.int32),
        jax.ShapeDtypeStruct((2, *pattern.shape), jnp.int32),
        jax.ShapeDtypeStruct((2, *rhs.shape[1:]), jnp.float32),
        jax.ShapeDtypeStruct(pivots.shape, pivots.dtype),
    )
    panel, urow, pmask, umask, smask, ybuf, pivots = pl.pallas_call(
        gather_kernel,
        out_shape=out_shape,
        in_specs=[pl.BlockSpec(memory_space=pltpu.HBM)] * 4,
        out_specs=[pl.BlockSpec(memory_space=pltpu.VMEM)] * 7,
        scratch_shapes=[
            dma((2, 4, 4)), dma((2, row_blocks * per)), dma((8,)),
            dma((col_blocks + per,)), dma((col_blocks + per,)),
            dma((col_blocks + per,)), dma((col_blocks + per,)),
            dma((2, 4)), dma((2,)), dma((1, 3)), dma((3,)), dma((3,)), dma((3,)),
        ],
        compiler_params=pltpu.CompilerParams(
            collective_id=0, has_side_effects=True, vmem_limit_bytes=16 * 2**20
        ),
        name="gather",
    )(blocks, pattern, rhs, pivots)
    return panel.reshape(2, row_blocks, side, side), urow, pmask, umask, smask, ybuf, pivots


def pieces(y):
    high = y.astype(jnp.bfloat16)
    rest = y - high.astype(jnp.float32)
    middle = rest.astype(jnp.bfloat16)
    low = (rest - middle.astype(jnp.float32)).astype(jnp.bfloat16)
    return high, middle, low


def matvec(stack, lower):
    return lax.dot_general(stack, lower, (((1,), (1,)), ((), ())), preferred_element_type=jnp.float32)


GROUP = 2


def update_kernel(
    pattern, pmask, umask, smask, blocks, panel, urow, pivots, ybuf, rhs, out, forward,
    lower, upper, corner, ystack, solved, stage, out_sem, forward_sem,
):
    row_blocks, side = blocks.shape[0], blocks.shape[2]
    col_blocks = urow.shape[1] - 1
    rows, cols = lax.axis_index("rows"), lax.axis_index("cols")
    f32, bf16 = jnp.float32, jnp.bfloat16
    dirs = rhs.shape[1]
    groups = [range(n, n + GROUP) for n in range(0, row_blocks, GROUP)]

    def product(left, right):
        return jnp.dot(left, right, preferred_element_type=f32)

    def keep(flag, value):
        return jnp.where(flag, value, jnp.zeros_like(value))

    def part(group):
        return pl.ds(group[0] * side, GROUP * side)

    def stacked(p, group):
        return panel[p, pl.ds(group[0], GROUP)].reshape(GROUP * side, side)

    left, right = pl.ds(0, side), pl.ds(side, side)

    corner[...] = keep(smask[0, 0, 0] == 1, urow[0, col_blocks])
    for group in groups:
        value = product(stacked(0, group), pivots[0]).astype(bf16)
        for n, i in enumerate(group):
            flag = jnp.logical_and(pmask[0, 0, i] == 1, i * 8 + rows > 0)
            lower[pl.ds(i * side, side), left] = keep(flag, value[n * side : (n + 1) * side])
    for group in groups:
        value = stacked(1, group).astype(f32) - product(lower[part(group), left], corner[...])
        lower[part(group), right] = value.astype(bf16)
    for group in groups:
        value = product(lower[part(group), right], pivots[1]).astype(bf16)
        for n, i in enumerate(group):
            flag = jnp.logical_and(pmask[1, 0, i] == 1, i * 8 + rows > 1)
            lower[pl.ds(i * side, side), right] = keep(flag, value[n * side : (n + 1) * side])
    lower_one = product(keep(smask[1, 0, 0] == 1, urow[1, col_blocks]), pivots[0]).astype(bf16)
    for c in range(col_blocks):
        first = keep(jnp.logical_and(umask[0, c, 0] == 1, c * 16 + cols > 0), urow[0, c])
        second = (urow[1, c].astype(f32) - product(lower_one, first)).astype(bf16)
        upper[c, left] = first
        upper[c, right] = keep(jnp.logical_and(umask[1, c, 0] == 1, c * 16 + cols > 1), second)
    ystack[...] = jnp.zeros_like(ystack)
    for n, piece in enumerate(pieces(ybuf[0])):
        ystack[pl.ds(8 * n, dirs), left] = piece.astype(f32)
    moved = matvec(ystack[:, left].astype(bf16), lower_one)
    taken = moved[0:dirs] + moved[8 : 8 + dirs] + moved[16 : 16 + dirs]
    for n, piece in enumerate(pieces(ybuf[1] - taken)):
        ystack[pl.ds(8 * n, dirs), right] = piece.astype(f32)
    def send(j, group):
        rows_of = pl.ds(group[0], GROUP)
        pltpu.make_async_copy(stage.at[j % 2, rows_of], out.at[rows_of, j], out_sem.at[j % 2]).start()

    def sent(j):
        pltpu.make_async_copy(stage.at[j % 2], out.at[:, j], out_sem.at[j % 2]).wait()

    for j in range(col_blocks):
        if j >= 2:
            sent(j - 2)
        for group in groups:
            prod = product(lower[part(group)], upper[j])
            for n, i in enumerate(group):
                fresh = (blocks[i, j].astype(f32) - prod[n * side : (n + 1) * side]).astype(bf16)
                stage[j % 2, i] = keep(pattern[j, i] == 1, fresh)
            if j > 0:
                send(j, group)
        if j == 0:
            for p in range(2):

                @pl.when(cols == p)
                def _():
                    for i in range(row_blocks):

                        @pl.when(i * 8 + rows > p)
                        def _():
                            stage[0, i] = lower[pl.ds(i * side, side), pl.ds(p * side, side)]

            for group in groups:
                send(j, group)
    for i in range(row_blocks):
        moved = matvec(ystack[...].astype(bf16), lower[pl.ds(i * side, side)])
        solved[i] = rhs[i] - (moved[0:dirs] + moved[8 : 8 + dirs] + moved[16 : 16 + dirs])
    send_forward = pltpu.make_async_copy(solved, forward, forward_sem)
    send_forward.start()
    sent(col_blocks - 2)
    sent(col_blocks - 1)
    send_forward.wait()


def update(blocks, pattern, rhs, panel, urow, pmask, umask, smask, ybuf, pivots):
    row_blocks, col_blocks, side = blocks.shape[:3]
    smem, vmem = pl.BlockSpec(memory_space=pltpu.SMEM), pl.BlockSpec(memory_space=pltpu.VMEM)
    return pl.pallas_call(
        update_kernel,
        out_shape=(
            jax.ShapeDtypeStruct(blocks.shape, blocks.dtype),
            jax.ShapeDtypeStruct(rhs.shape, rhs.dtype),
        ),
        in_specs=[smem] * 4 + [vmem] * 6,
        out_specs=[pl.BlockSpec(memory_space=pltpu.HBM)] * 2,
        scratch_shapes=[
            pltpu.VMEM((row_blocks * side, 2 * side), jnp.bfloat16),
            pltpu.VMEM((col_blocks, 2 * side, side), jnp.bfloat16),
            pltpu.VMEM((side, side), jnp.bfloat16),
            pltpu.VMEM((32, 2 * side), jnp.float32),
            pltpu.VMEM(rhs.shape, rhs.dtype),
            pltpu.VMEM((2, row_blocks, side, side), jnp.bfloat16),
            pltpu.SemaphoreType.DMA((2,)),
            pltpu.SemaphoreType.DMA,
        ],
        compiler_params=pltpu.CompilerParams(vmem_limit_bytes=24 * 2**20),
        name="update",
    )(pattern, pmask, umask, smask, blocks, panel, urow, pivots, ybuf, rhs)


def on_device(blocks, pattern, pivot_inverse, right_sides):
    pattern = pattern.T
    in_hbm = lambda array: pltpu.with_memory_space_constraint(array, pltpu.HBM)
    gathered = gather(in_hbm(blocks), in_hbm(pattern), in_hbm(right_sides), in_hbm(pivot_inverse))
    return tuple(update(blocks, pattern, right_sides, *gathered))


def solution(mesh):
    return jax.shard_map(
        on_device,
        mesh=mesh,
        in_specs=(P("rows", "cols", None, None), P("rows", "cols"), P(), P("rows", None, None)),
        out_specs=(P("rows", "cols", None, None), P("rows", None, None)),
        check_vma=False,
    )
```
